256 devices in a mesh: owner: 16 (over z, core), tensor: 16 (over x, y).
Axes of the slice: x: 4, y: 4, z: 8, core: 2. Of those that a mesh axis runs over, the one named last changes fastest.
Arguments:
- mixer_input: bfloat16 [16384, 2, 8192], P('owner', None, 'tensor'), may hold values from -6 to 6
- step_raw: float32 [16384, 128], P('owner', 'tensor'), may hold values from -7 to 5
- decay_rate: float32 [128], P('tensor'), may hold values from 0.005 to 0.5
- skip_gain: float32 [128], P('tensor'), may hold values from 0.5 to 2
- state_proj: bfloat16 [16384, 2, 4, 256], P('owner'), may hold values from -1.5 to 1.5
- queries: bfloat16 [16384, 4096], P('owner', 'tensor'), may hold values from -256 to 256
- suffix_kv: bfloat16 [16384, 2, 4, 128], P('owner'), may hold values from -6 to 6
- state_pool: bfloat16 [64, 128, 64, 256], P('owner', 'tensor'), may hold values from -1.5 to 1.5
- page_pool: bfloat16 [256, 128, 2, 4, 128], P('owner'), may hold values from -6 to 6
- norm_gain: float32 [8192], P('tensor'), may hold values from 0.1 to 1.9
- hit_owner: int32 [64, 1], replicated, may hold values from 0 to 15; in each aligned block of 4 rows (0 to 3, 4 to 7, ...) at most 2 rows name the same one
- hit_slot: int32 [64], replicated, may hold values from 0 to 3
- page_owner: int32 [64, 16, 1], replicated, may hold values from 0 to 15; in each aligned block of 64 rows (0 to 63, 64 to 127, ..., all dimensions but the last counted through in order) at most 6 rows name the same one
- page_slot: int32 [64, 16], replicated, may hold values from 0 to 15
- prefix_len: int32 [64], replicated, may hold values from 256 to 2048, as said below
- suffix_len: int32 [64], replicated, may hold values from 64 to 256, as said below
Outputs:
- mamba_out: bfloat16 [16384, 8192], P('owner', 'tensor')
- attn_out: bfloat16 [16384, 4096], P('owner', 'tensor')
The draws below stay inside these ranges and needn't reach their ends.
Inputs may be any that keep to these rules, and one draw needn't show every extreme that they name: `hit_owner`: the 4 requests on one index of owner name one owner at most 2 times, and some index reaches it. `page_owner`: of the 64 list entries of the requests on one index of owner, at most 6 name one owner, and some index reaches it. `prefix_len`: a multiple of 256; request 0 has 2048. `suffix_len`: request 0 has 256.
All inputs are finite; a program needn't handle non-finite values.
Results may differ from the reference program's by a relative error of at most 0.0045.
Values may be sent and summed in bfloat16 or wider, within the bound.
A program may use at most 192 MiB of HBM per device.

```python
import math
import jax
import jax.numpy as jnp
import numpy as np
from jax import lax

SSM_HEAD_TOTAL = 128
MHDIM = 64
STATE = 256
GROUPS = 4
QHEADS = 32
KVHEADS = 4
HD = 128
PAGE = 128
SPAN = 128
CKPT = 256
SUF = 256
PREFIX_MAX = 2048
REQ_DEV = 4
SLOTS_DEV = 4
PAGES_DEV = 16
CAP_S = 2
MAXP = 16
CAP_P = 6
REQS = 64
TRAILING_PLACES = 16384
SLOTS = 64
PAGES = 256
N_OWNER = 16


def draw_queries(key, part):
    start_shift = jnp.clip(jax.random.normal(key, (TRAILING_PLACES, QHEADS * HD), jnp.float32), -4.0, 4.0)
    return start_shift.astype(jnp.bfloat16)


def draw_step_raw(key, part):
    first_key, tiebreak_order = jax.random.split(key)
    start_shift = jnp.clip(jax.random.normal(first_key, (TRAILING_PLACES, SSM_HEAD_TOTAL), jnp.float32), -3.0, 3.0) - 2.5
    batch_lines = jax.random.randint(tiebreak_order, (TRAILING_PLACES, SSM_HEAD_TOTAL), 0, 48) == 0
    return (start_shift + jnp.where(batch_lines, 4.5, 0.0)).astype(jnp.float32)


def draw_prefix_len(key, part):
    counts = jax.random.randint(key, (REQS,), 1, PREFIX_MAX // CKPT + 1)
    counts = counts.at[0].set(PREFIX_MAX // CKPT)
    return (counts * CKPT).astype(jnp.int32)


def draw_suffix_len(key, part):
    lengths = jax.random.randint(key, (REQS,), SUF // 4, SUF + 1)
    lengths = lengths.at[0].set(SUF)
    return lengths.astype(jnp.int32)


def plant(values, own_key, low, high):
    longest = values.shape.index(max(values.shape))
    spots = []
    for shift in (0, 1):
        where = [jax.random.randint(jax.random.fold_in(own_key, axis), (), 0, length) for axis, length in enumerate(values.shape)]
        where[longest] = (where[longest] + shift) % values.shape[longest]
        spots.append(tuple(where))
    return values.at[spots[0]].set(low).at[spots[1]].set(high)


def shard_levels(key, shape, cuts, low, largest):
    def one(dim, blocks):
        draws = jax.random.uniform(jax.random.fold_in(jax.random.fold_in(key, 6), dim), (blocks,), jnp.float32, low / len(cuts), largest / len(cuts))
        return jnp.repeat(jnp.exp(draws), shape[dim] // blocks).reshape((-1,) + (1,) * (len(shape) - dim - 1))

    gain = one(*cuts[0])
    for cut in cuts[1:]:
        gain = gain * one(*cut)
    return gain


def shared_out(key, own, number, rows, count, top, bound, slope):
    sequence = jax.random.permutation(key, count)
    heavy_load, common = shares(count, rows * top, bound, slope, True), shares(count, rows * top, bound, slope, False)
    places = jnp.arange(count)

    def named(sizes, rotation):
        used = int((sizes > 0).sum())
        fixed = max(1, used // 4)
        shifted = fixed + (places - fixed + rotation * (used - fixed)) % max(1, count - fixed)
        return jnp.zeros((count,), jnp.int32).at[sequence[jnp.where(places < fixed, places, shifted)]].set(jnp.asarray(sizes, jnp.int32))

    sizes = jnp.where(number % 4 == 0, named(heavy_load, number // 4), named(common, number - number // 4 - 1))
    mixed = jax.random.permutation(jax.random.fold_in(own, 3), count)
    giver, receiver = mixed[0:count // 2 * 2:2], mixed[1:count // 2 * 2:2]
    margin = jnp.minimum(sizes[giver] - 1, bound - sizes[receiver]) // 2
    margin = jnp.where((giver == sequence[0]) | (receiver == sequence[0]) | (sizes[receiver] == 0), 0, jnp.maximum(margin, 0))
    shifted = jax.random.randint(jax.random.fold_in(own, 4), (count // 2,), 0, 1 << 20) % (margin + 1)
    sizes = sizes.at[giver].add(-shifted).at[receiver].add(shifted)
    labels = jnp.searchsorted(jnp.cumsum(sizes), jnp.arange(rows * top), side="right").astype(jnp.int32)
    table = labels.reshape(top, rows).T
    table = table[jax.random.permutation(jax.random.fold_in(own, 1), rows)]
    rotation = jax.random.randint(jax.random.fold_in(own, 2), (rows, 1), 0, top)
    return jnp.take_along_axis(table, (jnp.arange(top)[None, :] + rotation) % top, axis=1)


def shares(count, total, most, slope, full):
    weights = [(1 << 20) // math.isqrt(grade ** slope) + 1 for grade in range(1, count + 1)]
    largest = most if full else min(most, max(-(-total // count), total * weights[0] // sum(weights)))
    least = 1 if total - largest >= count - 1 else 0
    given, spare = [largest] + [least] * (count - 1), total - largest - least * (count - 1)
    while spare > 0:
        candidates = [i for i in range(1, count) if given[i] < largest] or [i for i in range(1, count) if given[i] < most]
        whole, left = sum([weights[i] for i in candidates]), spare
        for i in candidates:
            extra = min(most - given[i], max(1, left * weights[i] // whole), spare)
            given[i] = given[i] + extra
            spare = spare - extra
    return np.array(given)


def noise(own_key, shape, deviation, bound, cuts=(), kind=jnp.bfloat16):
    level = shard_levels(own_key, shape, cuts, -0.22, 0.18) if cuts else 1.0
    values = jax.random.normal(own_key, shape, jnp.float32) * deviation * level
    return jnp.minimum(jnp.maximum(values, -bound), bound).astype(kind)


def setup_inputs(seed: int = 0) -> dict:
    splits = jax.random.split(jax.random.key(seed), 17)
    mixer_input = noise(splits[0], (TRAILING_PLACES, 2, SSM_HEAD_TOTAL * MHDIM), 1.0, 6.0, ((0, 16), (2, 16)))
    step_raw = draw_step_raw(jax.random.fold_in(splits[16], 71), 0)
    decay_rate = jnp.clip(jnp.exp(math.log(0.5) - 4.6051702 * jax.random.uniform(splits[2], (SSM_HEAD_TOTAL,), jnp.float32) ** shard_levels(splits[2], (SSM_HEAD_TOTAL,), ((0, 16),), -0.2, 0.2)), 0.005, 0.5)
    skip_gain = jnp.clip(0.5 + 1.5 * jax.random.uniform(splits[3], (SSM_HEAD_TOTAL,), jnp.float32) ** shard_levels(splits[3], (SSM_HEAD_TOTAL,), ((0, 16),), -0.2, 0.2), 0.5, 2.0)
    state_proj = noise(splits[4], (TRAILING_PLACES, 2, GROUPS, STATE), 0.25, 1.5, ((0, 16),))
    queries = draw_queries(jax.random.fold_in(splits[16], 71), 0)
    suffix_kv = noise(splits[6], (TRAILING_PLACES, 2, KVHEADS, HD), 1.0, 6.0, ((0, 16),))
    state_pool = noise(splits[7], (SLOTS, SSM_HEAD_TOTAL, MHDIM, STATE), 0.25, 1.5, ((0, 16), (1, 16)))
    page_pool = noise(splits[8], (PAGES, PAGE, 2, KVHEADS, HD), 1.0, 6.0, ((0, 16),))
    norm_gain = jnp.clip(1.0 + 0.18 * jax.random.normal(splits[9], (SSM_HEAD_TOTAL * MHDIM,), jnp.float32), 0.1, 1.9)
    hit_owner_keys = jax.random.split(jax.random.fold_in(splits[10], 1), REQS // REQ_DEV)
    hit_owner_turns = jax.random.permutation(jax.random.fold_in(splits[10], 3), REQS // REQ_DEV)
    hit_owner = jax.vmap(lambda own, number: shared_out(jax.random.fold_in(splits[10], 2), own, number, REQ_DEV, N_OWNER, 1, CAP_S, 2))(hit_owner_keys, hit_owner_turns).reshape((REQS, 1))
    hit_slot = plant(jax.random.randint(splits[11], (REQS,), 0, SLOTS_DEV), jax.random.fold_in(splits[11], 1), 0, SLOTS_DEV - 1).astype(jnp.int32)
    page_owner_keys = jax.random.split(jax.random.fold_in(splits[12], 1), REQS * MAXP // (REQ_DEV * MAXP))
    page_owner_turns = jax.random.permutation(jax.random.fold_in(splits[12], 3), REQS * MAXP // (REQ_DEV * MAXP))
    page_owner = jax.vmap(lambda own, number: shared_out(jax.random.fold_in(splits[12], 2), own, number, REQ_DEV * MAXP, N_OWNER, 1, CAP_P, 2))(page_owner_keys, page_owner_turns).reshape((REQS, MAXP, 1))
    page_slot = plant(jax.random.randint(splits[13], (REQS, MAXP), 0, PAGES_DEV), jax.random.fold_in(splits[13], 1), 0, PAGES_DEV - 1).astype(jnp.int32)
    prefix_len = draw_prefix_len(jax.random.fold_in(splits[16], 71), 0)
    suffix_len = draw_suffix_len(jax.random.fold_in(splits[16], 71), 0)
    return {"mixer_input": mixer_input, "step_raw": step_raw, "decay_rate": decay_rate, "skip_gain": skip_gain, "state_proj": state_proj, "queries": queries, "suffix_kv": suffix_kv, "state_pool": state_pool, "page_pool": page_pool, "norm_gain": norm_gain, "hit_owner": hit_owner, "hit_slot": hit_slot, "page_owner": page_owner, "page_slot": page_slot, "prefix_len": prefix_len, "suffix_len": suffix_len}


EPSILON = 1e-05
NEG_FILL = -1e+30

def half(value):
    return lax.optimization_barrier(value.astype(jnp.bfloat16)).astype(jnp.float32)

def mixer_core(x_heads, z_heads, rate_raw, decay_groups, skip_groups, b_rows, c_rows, start_state):
    seq_len, group_count, head_count, head_width = x_heads.shape
    blocks = seq_len // SPAN
    step_rate = jax.nn.softplus(rate_raw)
    keep_log = -step_rate * decay_groups[None]
    x_block = x_heads.reshape(blocks, SPAN, group_count, head_count, head_width).astype(jnp.float32)
    rate_block = step_rate.reshape(blocks, SPAN, group_count, head_count)
    cum_block = jnp.cumsum(keep_log.reshape(blocks, SPAN, group_count, head_count), axis=1)
    b_block = b_rows.reshape(blocks, SPAN, group_count, -1).astype(jnp.float32)
    c_block = c_rows.reshape(blocks, SPAN, group_count, -1).astype(jnp.float32)
    intersection = jnp.einsum('cign,cjgn->cgij', c_block, b_block)
    cum_moved = jnp.transpose(cum_block, (0, 2, 3, 1))
    rate_moved = jnp.transpose(rate_block, (0, 2, 3, 1))
    lower = jnp.arange(SPAN)[:, None] >= jnp.arange(SPAN)[None, :]
    fade = jnp.exp(jnp.where(lower, cum_moved[..., :, None] - cum_moved[..., None, :], NEG_FILL))
    weights = half(intersection[:, :, None] * fade * rate_moved[..., None, :])
    inner = jnp.einsum('cghij,cjghp->cighp', weights, x_block)
    cum_end = cum_block[:, -1]
    tail = jnp.exp(cum_end[:, None] - cum_block) * rate_block
    scaled = half(tail[..., None] * x_block)
    block_state = jnp.einsum('cjghp,cjgn->cghpn', scaled, b_block)
    carry = start_state.astype(jnp.float32)
    begins = []
    for block_index in range(blocks):
        begins.append(carry)
        carry = jnp.exp(cum_end[block_index])[..., None, None] * carry + block_state[block_index]
    begin_half = half(jnp.stack(begins))
    carried = jnp.einsum('cign,cghpn->cighp', c_block, begin_half)
    summed = inner + jnp.exp(cum_block)[..., None] * carried + skip_groups[None, None, :, :, None] * x_block
    gate = jax.nn.silu(z_heads.astype(jnp.float32)).reshape(blocks, SPAN, group_count, head_count, head_width)
    return (summed * gate).reshape(seq_len, group_count, head_count, head_width)

def attend(query, key_pre, value_pre, key_suf, value_suf, prefix_count):
    softmax_scale = 1.0 / math.sqrt(HD)
    query_wide = query.astype(jnp.float32)
    score_pre = jnp.einsum('qhd,md->hqm', query_wide, key_pre.astype(jnp.float32)) * softmax_scale
    score_suf = jnp.einsum('qhd,kd->hqk', query_wide, key_suf.astype(jnp.float32)) * softmax_scale
    pre_live = jnp.arange(key_pre.shape[0]) < prefix_count
    causal = jnp.arange(SUF)[:, None] >= jnp.arange(SUF)[None, :]
    score_pre = jnp.where(pre_live[None, None, :], score_pre, NEG_FILL)
    score_suf = jnp.where(causal[None], score_suf, NEG_FILL)
    row_max = jnp.maximum(lax.optimization_barrier(jnp.max(score_pre, axis=2)), lax.optimization_barrier(jnp.max(score_suf, axis=2)))
    weight_pre = jnp.exp(score_pre - row_max[..., None])
    weight_suf = jnp.exp(score_suf - row_max[..., None])
    denominator = lax.optimization_barrier(jnp.sum(weight_pre, axis=2)) + lax.optimization_barrier(jnp.sum(weight_suf, axis=2))
    mixed = jnp.einsum('hqm,md->qhd', half(weight_pre), value_pre.astype(jnp.float32))
    mixed = mixed + jnp.einsum('hqk,kd->qhd', half(weight_suf), value_suf.astype(jnp.float32))
    return mixed / jnp.transpose(denominator)[:, :, None]

def reference(mixer_input, step_raw, decay_rate, skip_gain, state_proj, queries, suffix_kv, state_pool, page_pool, norm_gain, hit_owner, hit_slot, page_owner, page_slot, prefix_len, suffix_len):
    per_group = SSM_HEAD_TOTAL // GROUPS
    per_kv = QHEADS // KVHEADS
    decay_groups = decay_rate.reshape(GROUPS, per_group)
    skip_groups = skip_gain.reshape(GROUPS, per_group)
    gain_groups = norm_gain.reshape(GROUPS, per_group, MHDIM)
    positions = jnp.arange(SUF)

    def one_request(request):
        first_row = (request * SUF).astype(jnp.int32)
        rows_input = lax.dynamic_slice_in_dim(mixer_input, first_row, SUF, 0)
        x_heads = rows_input[:, 0].reshape(SUF, GROUPS, per_group, MHDIM)
        z_heads = rows_input[:, 1].reshape(SUF, GROUPS, per_group, MHDIM)
        rate_raw = lax.dynamic_slice_in_dim(step_raw, first_row, SUF, 0).reshape(SUF, GROUPS, per_group)
        line_targets = lax.dynamic_slice_in_dim(state_proj, first_row, SUF, 0)
        start_index = (hit_owner[request, 0] * SLOTS_DEV + hit_slot[request]).astype(jnp.int32)
        start_state = lax.dynamic_index_in_dim(state_pool, start_index, 0, keepdims=False)
        start_state = start_state.reshape(GROUPS, per_group, MHDIM, STATE)
        gated = mixer_core(x_heads, z_heads, rate_raw, decay_groups, skip_groups, line_targets[:, 0], line_targets[:, 1], start_state)
        square = lax.optimization_barrier(jnp.sum(gated * gated, axis=(2, 3))) / (per_group * MHDIM)
        rescaled_input = gated * lax.rsqrt(square + EPSILON)[:, :, None, None] * gain_groups[None]
        active = positions < suffix_len[request]
        mamba_rows = jnp.where(active[:, None], rescaled_input.reshape(SUF, SSM_HEAD_TOTAL * MHDIM), 0.0).astype(jnp.bfloat16)
        page_index = (page_owner[request, :, 0] * PAGES_DEV + page_slot[request]).astype(jnp.int32)
        prefix_kv = jnp.take(page_pool, page_index, axis=0).reshape(MAXP * PAGE, 2, KVHEADS, HD)
        rows_kv = lax.dynamic_slice_in_dim(suffix_kv, first_row, SUF, 0)
        query = lax.dynamic_slice_in_dim(queries, first_row, SUF, 0).reshape(SUF, KVHEADS, per_kv, HD)
        mixed = jax.vmap(attend, in_axes=(1, 1, 1, 1, 1, None), out_axes=1)(query, prefix_kv[:, 0], prefix_kv[:, 1], rows_kv[:, 0], rows_kv[:, 1], prefix_len[request])
        attn_rows = jnp.where(active[:, None], mixed.reshape(SUF, QHEADS * HD), 0.0).astype(jnp.bfloat16)
        return (mamba_rows, attn_rows)
    mamba_all, attn_all = lax.map(one_request, jnp.arange(REQS, dtype=jnp.int32))
    return (mamba_all.reshape(TRAILING_PLACES, SSM_HEAD_TOTAL * MHDIM), attn_all.reshape(TRAILING_PLACES, QHEADS * HD))
```

```python
import functools
import math

import jax
import jax.numpy as jnp
from jax import lax
from jax.experimental import pallas as pl
from jax.experimental.pallas import tpu as pltpu
from jax.sharding import Mesh
from jax.sharding import PartitionSpec as P

HEADS = 8
MHDIM = 64
CH = HEADS * MHDIM
STATE = 256
GROUP_CH = 2048
HD = 128
PAGE = 128
SPAN = 128
SUF = 256
MAXP = 16
REQ = 4
QUARTER = PAGE // 4
EPSILON = 1e-05
NEG = -1e30
OWN = ("z", "core")
BF = jnp.bfloat16
F32 = jnp.float32
HI = lax.Precision.HIGHEST


def dot_nt(a, b):
    return lax.dot_general(a, b, (((1,), (1,)), ((), ())), preferred_element_type=F32)


def dot_nn(a, b):
    return lax.dot_general(a, b, (((1,), (0,)), ((), ())), preferred_element_type=F32)


def dot_tn(a, b):
    return lax.dot_general(a, b, (((0,), (0,)), ((), ())), preferred_element_type=F32)


def expand(cols):
    head = lax.broadcasted_iota(jnp.int32, (HEADS, CH), 0)
    chan = lax.broadcasted_iota(jnp.int32, (HEADS, CH), 1)
    pick = (chan // MHDIM == head).astype(F32)
    return lax.dot_general(
        cols, pick, (((1,), (0,)), ((), ())), preferred_element_type=F32, precision=HI
    )


def mixer_local_kernel(x_ref, z_ref, step_ref, decay_ref, skip_ref, b_ref, c_ref, p_ref, e_ref, bs_ref, dec_ref):
    lane = lax.broadcasted_iota(jnp.int32, (HEADS, SPAN), 1)
    row = lax.broadcasted_iota(jnp.int32, (SPAN, SPAN), 0)
    col = lax.broadcasted_iota(jnp.int32, (SPAN, SPAN), 1)
    lower = row >= col
    low_half = lax.broadcasted_iota(jnp.int32, (SPAN, 2 * MHDIM), 1) < MHDIM
    for blk in range(SUF // SPAN):
        rows = pl.ds(blk * SPAN, SPAN)
        raw = step_ref[:, rows]
        rate = jnp.maximum(raw, 0.0) + jnp.log(1.0 + jnp.exp(-jnp.abs(raw)))
        cum = -rate * decay_ref[...]
        shift = 1
        while shift < SPAN:
            cum = cum + jnp.where(lane >= shift, pltpu.roll(cum, shift, 1), 0.0)
            shift *= 2
        cum_col = jnp.transpose(cum)
        x = x_ref[rows, :]
        b = b_ref[rows, :]
        c = c_ref[rows, :]
        inter = dot_nt(c, b)
        for pair in range(HEADS // 2):
            parts = []
            for h in (2 * pair, 2 * pair + 1):
                gap = cum_col[:, h : h + 1] - cum[h : h + 1, :]
                fade = jnp.exp(jnp.where(lower, gap, NEG))
                parts.append((inter * fade * rate[h : h + 1, :]).astype(BF))
            lanes = pl.ds(pair * 2 * MHDIM, 2 * MHDIM)
            xp = x_ref[rows, lanes]
            first = dot_nn(parts[0], xp)
            second = dot_nn(parts[1], xp)
            inner = jnp.where(low_half, first, second)
            z = z_ref[rows, lanes].astype(F32)
            gate = z / (1.0 + jnp.exp(-z))
            p_ref[rows, lanes] = (inner + skip_ref[:, lanes] * xp.astype(F32)) * gate
            grow = jnp.where(
                low_half,
                jnp.broadcast_to(cum_col[:, 2 * pair : 2 * pair + 1], (SPAN, 2 * MHDIM)),
                jnp.broadcast_to(cum_col[:, 2 * pair + 1 : 2 * pair + 2], (SPAN, 2 * MHDIM)),
            )
            e_ref[rows, lanes] = jnp.exp(grow) * gate
        if blk == 0:
            end = cum[:, SPAN - 1 : SPAN]
            tail = jnp.transpose(jnp.exp(end - cum) * rate)
            scaled = (expand(tail) * x.astype(F32)).astype(BF)
            bs_ref[...] = dot_tn(scaled, b)
            keep = jnp.transpose(jnp.broadcast_to(jnp.exp(end), (HEADS, SPAN)))
            dec_ref[...] = jnp.transpose(expand(keep))


def mixer_local(x, z, step_t, decay, skip, b, c):
    tok = x.shape[0]
    return pl.pallas_call(
        mixer_local_kernel,
        grid=(REQ,),
        in_specs=[
            pl.BlockSpec((SUF, CH), lambda i: (i, 0)),
            pl.BlockSpec((SUF, CH), lambda i: (i, 0)),
            pl.BlockSpec((HEADS, SUF), lambda i: (0, i)),
            pl.BlockSpec((HEADS, 1), lambda i: (0, 0)),
            pl.BlockSpec((1, CH), lambda i: (0, 0)),
            pl.BlockSpec((SUF, STATE), lambda i: (i, 0)),
            pl.BlockSpec((SUF, STATE), lambda i: (i, 0)),
        ],
        out_specs=[
            pl.BlockSpec((SUF, CH), lambda i: (i, 0)),
            pl.BlockSpec((SUF, CH), lambda i: (i, 0)),
            pl.BlockSpec((None, CH, STATE), lambda i: (i, 0, 0)),
            pl.BlockSpec((None, CH, SPAN), lambda i: (i, 0, 0)),
        ],
        out_shape=[
            jax.ShapeDtypeStruct((tok, CH), F32),
            jax.ShapeDtypeStruct((tok, CH), F32),
            jax.ShapeDtypeStruct((REQ, CH, STATE), F32),
            jax.ShapeDtypeStruct((REQ, CH, SPAN), F32),
        ],
        compiler_params=pltpu.CompilerParams(vmem_limit_bytes=24 << 20),
        cost_estimate=pl.CostEstimate(flops=2_000_000_000, bytes_accessed=11 << 20, transcendentals=2 << 20),
        name="mixer_local",
    )(x, z, step_t, decay, skip, b, c)


def mixer_state_kernel(s_ref, c_ref, p_ref, e_ref, bs_ref, dec_ref, g_ref, sq_ref):
    start = s_ref[...].reshape(CH, STATE)
    dec = dec_ref[...]
    begin = jnp.concatenate([dec, dec], axis=1) * start.astype(F32) + bs_ref[...]
    sums = []
    for blk, state in enumerate((start, begin.astype(BF))):
        rows = pl.ds(blk * SPAN, SPAN)
        carried = dot_nt(c_ref[rows, :], state)
        gated = p_ref[rows, :] + e_ref[rows, :] * carried
        g_ref[rows, :] = gated
        sums.append(jnp.sum(gated * gated, axis=1, keepdims=True))
    sq_ref[...] = jnp.concatenate(sums, axis=0)


def mixer_state(states, c, p, e, bs, dec):
    tok = c.shape[0]
    return pl.pallas_call(
        mixer_state_kernel,
        grid=(REQ,),
        in_specs=[
            pl.BlockSpec((16, None, CH // 16, STATE), lambda i: (0, i, 0, 0)),
            pl.BlockSpec((SUF, STATE), lambda i: (i, 0)),
            pl.BlockSpec((SUF, CH), lambda i: (i, 0)),
            pl.BlockSpec((SUF, CH), lambda i: (i, 0)),
            pl.BlockSpec((None, CH, STATE), lambda i: (i, 0, 0)),
            pl.BlockSpec((None, CH, SPAN), lambda i: (i, 0, 0)),
        ],
        out_specs=[
            pl.BlockSpec((SUF, CH), lambda i: (i, 0)),
            pl.BlockSpec((SUF, 1), lambda i: (i, 0)),
        ],
        out_shape=[
            jax.ShapeDtypeStruct((tok, CH), F32),
            jax.ShapeDtypeStruct((tok, 1), F32),
        ],
        compiler_params=pltpu.CompilerParams(vmem_limit_bytes=24 << 20),
        cost_estimate=pl.CostEstimate(flops=600_000_000, bytes_accessed=11 << 20, transcendentals=0),
        name="mixer_state",
    )(states, c, p, e, bs, dec)


def attend_kernel(pre_ref, suf_ref, base_ref, q_ref, kv_ref, ks_ref, vs_ref, o_ref):
    req = base_ref[0]
    keys = MAXP * PAGE
    q = q_ref[...]
    kv = kv_ref[...].reshape(4 * MAXP, 2 * QUARTER, HD)
    k = kv[:, :QUARTER, :].reshape(keys, HD)
    v = kv[:, QUARTER:, :].reshape(keys, HD)
    scale = 1.0 / math.sqrt(HD)
    s_pre = dot_nt(q, k) * scale
    s_suf = dot_nt(q, ks_ref[...]) * scale
    page = (lax.broadcasted_iota(jnp.int32, (1, keys), 1) // QUARTER) % MAXP
    s_pre = jnp.where(page * PAGE < pre_ref[req], s_pre, NEG)
    row = lax.broadcasted_iota(jnp.int32, (SUF, SUF), 0)
    col = lax.broadcasted_iota(jnp.int32, (SUF, SUF), 1)
    s_suf = jnp.where(row >= col, s_suf, NEG)
    top = jnp.maximum(
        jnp.max(s_pre, axis=1, keepdims=True), jnp.max(s_suf, axis=1, keepdims=True)
    )
    w_pre = jnp.exp(s_pre - top)
    w_suf = jnp.exp(s_suf - top)
    total = jnp.sum(w_pre, axis=1, keepdims=True) + jnp.sum(w_suf, axis=1, keepdims=True)
    mixed = dot_nn(w_pre.astype(BF), v) + dot_nn(w_suf.astype(BF), vs_ref[...])
    out = mixed / total
    live = lax.broadcasted_iota(jnp.int32, (SUF, HD), 0) < suf_ref[req]
    o_ref[...] = jnp.where(live, out, 0.0).astype(BF)


def attend(prefix_len, suffix_len, base, q, kv, ks, vs):
    return pl.pallas_call(
        attend_kernel,
        grid_spec=pltpu.PrefetchScalarGridSpec(
            num_scalar_prefetch=3,
            grid=(8,),
            in_specs=[
                pl.BlockSpec((None, SUF, HD), lambda h, *_: (h // 2, 0, h % 2)),
                pl.BlockSpec((4, MAXP, 2 * QUARTER, HD), lambda h, *_: (0, 0, 0, 0)),
                pl.BlockSpec((SUF, HD), lambda h, *_: (0, 0)),
                pl.BlockSpec((SUF, HD), lambda h, *_: (0, 0)),
            ],
            out_specs=pl.BlockSpec((None, SUF, HD), lambda h, *_: (h // 2, 0, h % 2)),
        ),
        out_shape=jax.ShapeDtypeStruct((4, SUF, 2 * HD), BF),
        compiler_params=pltpu.CompilerParams(vmem_limit_bytes=32 << 20),
        cost_estimate=pl.CostEstimate(flops=2_400_000_000, bytes_accessed=3 << 20, transcendentals=5 << 20),
        name="attend",
    )(prefix_len, suffix_len, base, q, kv, ks, vs)


def gather_kernel(count, base_scale, per, own_ref, slot_ref, base_ref, src_ref, dst_ref, sem):
    first = base_ref[0] * base_scale

    def begin(i, carry):
        e = first + i
        pltpu.make_async_copy(src_ref.at[own_ref[e] * per + slot_ref[e]], dst_ref.at[i], sem).start()
        return carry

    lax.fori_loop(0, count, begin, 0)
    pltpu.make_async_copy(src_ref.at[pl.ds(0, count)], dst_ref, sem).wait()


def gather(owner, slot, base, base_scale, per, table, count, name):
    return pl.pallas_call(
        functools.partial(gather_kernel, count, base_scale, per),
        grid_spec=pltpu.PrefetchScalarGridSpec(
            num_scalar_prefetch=3,
            grid=(1,),
            in_specs=[pl.BlockSpec(memory_space=pl.ANY)],
            out_specs=pl.BlockSpec(memory_space=pl.ANY),
            scratch_shapes=[pltpu.SemaphoreType.DMA(())],
        ),
        out_shape=jax.ShapeDtypeStruct((count,) + table.shape[1:], table.dtype),
        cost_estimate=pl.CostEstimate(flops=0, bytes_accessed=2 << 20, transcendentals=0),
        name=name,
    )(owner, slot, base, table)


def body(
    mixer_input,
    step_raw,
    decay_rate,
    skip_gain,
    state_proj,
    queries,
    suffix_kv,
    state_pool,
    page_pool,
    norm_gain,
    hit_owner,
    hit_slot,
    page_owner,
    page_slot,
    prefix_len,
    suffix_len,
):
    owner_index = lax.axis_index("z") * 2 + lax.axis_index("core")
    x_index = lax.axis_index("x")
    y_index = lax.axis_index("y")
    tok = REQ * SUF

    piece = lax.dynamic_slice(
        page_pool, (0, y_index * QUARTER, 0, x_index, 0), (16, QUARTER, 2, 1, HD)
    ).reshape(16, QUARTER, 2, HD)
    piece = jnp.transpose(piece, (0, 2, 1, 3)).reshape(16, 2 * QUARTER, HD)
    pool = lax.all_gather(piece, OWN, axis=0, tiled=True)

    cut = jnp.transpose(state_pool.reshape(4, 16, CH // 16, STATE), (1, 0, 2, 3))
    hop = lax.all_to_all(cut, OWN, split_axis=0, concat_axis=0, tiled=True)

    query = lax.all_to_all(queries.reshape(REQ, SUF, 2 * HD), "y", split_axis=0, concat_axis=0, tiled=True)

    x = mixer_input[:, 0]
    z = mixer_input[:, 1]
    maps = lax.dynamic_slice(state_proj, (0, 0, x_index, 0), (tok, 2, 1, STATE))
    b = maps[:, 0, 0]
    c = maps[:, 1, 0]
    skip = jnp.repeat(skip_gain, MHDIM)[None]
    p, e, bs, dec = mixer_local(x, z, step_raw.T, decay_rate[:, None], skip, b, c)

    zero = jnp.zeros((1,), jnp.int32)
    wanted = gather(
        hit_owner.reshape(-1), hit_slot, zero, 0, 4, hop.reshape(64, CH // 16, STATE), 64, "pick_states"
    )
    states = lax.all_to_all(wanted.reshape(16, REQ, CH // 16, STATE), OWN, split_axis=0, concat_axis=0, tiled=True)

    base = owner_index.astype(jnp.int32).reshape(1)
    mine = gather(
        page_owner.reshape(-1), page_slot.reshape(-1), base, REQ * MAXP, 16, pool, REQ * MAXP, "pick_pages"
    )
    kv = lax.all_to_all(mine.reshape(REQ, MAXP, 2 * QUARTER, HD), "y", split_axis=0, concat_axis=0, tiled=True)
    own_kv = lax.dynamic_slice(
        suffix_kv, (y_index * SUF, 0, x_index, 0), (SUF, 2, 1, HD)
    )
    request = base * REQ + y_index
    mixed = attend(prefix_len, suffix_len, request, query, kv, own_kv[:, 0, 0], own_kv[:, 1, 0])
    attn_out = lax.all_to_all(mixed, "y", split_axis=0, concat_axis=0, tiled=True).reshape(tok, 2 * HD)

    gated, sums = mixer_state(states, c, p, e, bs, dec)
    square = lax.psum(sums.reshape(8, tok // 8), "y").reshape(tok, 1) / GROUP_CH
    my_suffix = lax.dynamic_slice_in_dim(suffix_len, owner_index * REQ, REQ, 0)
    active = (jnp.arange(SUF)[None, :] < my_suffix[:, None]).reshape(-1)
    normed = gated * lax.rsqrt(square + EPSILON) * norm_gain[None, :]
    mamba_out = jnp.where(active[:, None], normed, 0.0).astype(BF)
    return (mamba_out, attn_out)


def solution(mesh):
    grid = Mesh(mesh.devices.reshape(8, 2, 4, 4), ("z", "core", "x", "y"))
    col = ("x", "y")
    return jax.shard_map(
        body,
        mesh=grid,
        in_specs=(
            P(OWN, None, col),
            P(OWN, col),
            P(col),
            P(col),
            P(OWN, None, None, None),
            P(OWN, col),
            P(OWN, None, None, None),
            P(OWN, col, None, None),
            P(OWN, None, None, None, None),
            P(col),
            P(),
            P(),
            P(),
            P(),
            P(),
            P(),
        ),
        out_specs=(P(OWN, col), P(OWN, col)),
        check_vma=False,
    )
```

```python
import functools
import math

import jax
import jax.numpy as jnp
from jax import lax
from jax.experimental import pallas as pl
from jax.experimental.pallas import tpu as pltpu
from jax.sharding import Mesh
from jax.sharding import PartitionSpec as P

HEADS = 8
MHDIM = 64
CH = HEADS * MHDIM
STATE = 256
GROUP_CH = 2048
HD = 128
PAGE = 128
SPAN = 128
SUF = 256
MAXP = 16
REQ = 4
QUARTER = PAGE // 4
EPSILON = 1e-05
NEG = -1e30
OWN = ("z", "core")
BF = jnp.bfloat16
F32 = jnp.float32
HI = lax.Precision.HIGHEST


def dot_nt(a, b):
    return lax.dot_general(a, b, (((1,), (1,)), ((), ())), preferred_element_type=F32)


def dot_nn(a, b):
    return lax.dot_general(a, b, (((1,), (0,)), ((), ())), preferred_element_type=F32)


def dot_tn(a, b):
    return lax.dot_general(a, b, (((0,), (0,)), ((), ())), preferred_element_type=F32)


def expand(cols):
    head = lax.broadcasted_iota(jnp.int32, (HEADS, CH), 0)
    chan = lax.broadcasted_iota(jnp.int32, (HEADS, CH), 1)
    pick = (chan // MHDIM == head).astype(F32)
    return lax.dot_general(
        cols, pick, (((1,), (0,)), ((), ())), preferred_element_type=F32, precision=HI
    )


def mixer_local_kernel(x_ref, z_ref, step_ref, decay_ref, skip_ref, b_ref, c_ref, p_ref, e_ref, bs_ref, dec_ref):
    lane = lax.broadcasted_iota(jnp.int32, (HEADS, SPAN), 1)
    row = lax.broadcasted_iota(jnp.int32, (SPAN, SPAN), 0)
    col = lax.broadcasted_iota(jnp.int32, (SPAN, SPAN), 1)
    lower = row >= col
    low_half = lax.broadcasted_iota(jnp.int32, (SPAN, 2 * MHDIM), 1) < MHDIM
    for blk in range(SUF // SPAN):
        rows = pl.ds(blk * SPAN, SPAN)
        raw = step_ref[:, rows]
        rate = jnp.maximum(raw, 0.0) + jnp.log(1.0 + jnp.exp(-jnp.abs(raw)))
        cum = -rate * decay_ref[...]
        shift = 1
        while shift < SPAN:
            cum = cum + jnp.where(lane >= shift, pltpu.roll(cum, shift, 1), 0.0)
            shift *= 2
        cum_col = jnp.transpose(cum)
        x = x_ref[rows, :]
        b = b_ref[rows, :]
        c = c_ref[rows, :]
        inter = dot_nt(c, b)
        for pair in range(HEADS // 2):
            parts = []
            for h in (2 * pair, 2 * pair + 1):
                gap = cum_col[:, h : h + 1] - cum[h : h + 1, :]
                fade = jnp.exp(jnp.where(lower, gap, NEG))
                parts.append((inter * fade * rate[h : h + 1, :]).astype(BF))
            lanes = pl.ds(pair * 2 * MHDIM, 2 * MHDIM)
            xp = x_ref[rows, lanes]
            first = dot_nn(parts[0], xp)
            second = dot_nn(parts[1], xp)
            inner = jnp.where(low_half, first, second)
            z = z_ref[rows, lanes].astype(F32)
            gate = z / (1.0 + jnp.exp(-z))
            p_ref[rows, lanes] = (inner + skip_ref[:, lanes] * xp.astype(F32)) * gate
            grow = jnp.where(
                low_half,
                jnp.broadcast_to(cum_col[:, 2 * pair : 2 * pair + 1], (SPAN, 2 * MHDIM)),
                jnp.broadcast_to(cum_col[:, 2 * pair + 1 : 2 * pair + 2], (SPAN, 2 * MHDIM)),
            )
            e_ref[rows, lanes] = jnp.exp(grow) * gate
        if blk == 0:
            end = cum[:, SPAN - 1 : SPAN]
            tail = jnp.transpose(jnp.exp(end - cum) * rate)
            scaled = (expand(tail) * x.astype(F32)).astype(BF)
            bs_ref[...] = dot_tn(scaled, b)
            keep = jnp.transpose(jnp.broadcast_to(jnp.exp(end), (HEADS, SPAN)))
            dec_ref[...] = jnp.transpose(expand(keep))


def mixer_local(x, z, step_t, decay, skip, b, c):
    tok = x.shape[0]
    return pl.pallas_call(
        mixer_local_kernel,
        grid=(REQ,),
        in_specs=[
            pl.BlockSpec((SUF, CH), lambda i: (i, 0)),
            pl.BlockSpec((SUF, CH), lambda i: (i, 0)),
            pl.BlockSpec((HEADS, SUF), lambda i: (0, i)),
            pl.BlockSpec((HEADS, 1), lambda i: (0, 0)),
            pl.BlockSpec((1, CH), lambda i: (0, 0)),
            pl.BlockSpec((SUF, STATE), lambda i: (i, 0)),
            pl.BlockSpec((SUF, STATE), lambda i: (i, 0)),
        ],
        out_specs=[
            pl.BlockSpec((SUF, CH), lambda i: (i, 0)),
            pl.BlockSpec((SUF, CH), lambda i: (i, 0)),
            pl.BlockSpec((None, CH, STATE), lambda i: (i, 0, 0)),
            pl.BlockSpec((None, CH, SPAN), lambda i: (i, 0, 0)),
        ],
        out_shape=[
            jax.ShapeDtypeStruct((tok, CH), F32),
            jax.ShapeDtypeStruct((tok, CH), F32),
            jax.ShapeDtypeStruct((REQ, CH, STATE), F32),
            jax.ShapeDtypeStruct((REQ, CH, SPAN), F32),
        ],
        compiler_params=pltpu.CompilerParams(vmem_limit_bytes=24 << 20),
        cost_estimate=pl.CostEstimate(flops=2_000_000_000, bytes_accessed=11 << 20, transcendentals=2 << 20),
        name="mixer_local",
    )(x, z, step_t, decay, skip, b, c)


MESH = pl.DeviceIdType.MESH


def attend_pair(q_ref, k, v, ks, vs, bias, causal, live, o_ref, slot):
    scale = 1.0 / math.sqrt(HD)
    for half in range(2):
        lanes = pl.ds(half * HD, HD)
        q = q_ref[slot, :, lanes]
        s_pre = dot_nt(q, k) * scale + bias
        s_suf = jnp.where(causal, dot_nt(q, ks) * scale, NEG)
        top = jnp.maximum(
            jnp.max(s_pre, axis=1, keepdims=True), jnp.max(s_suf, axis=1, keepdims=True)
        )
        w_pre = jnp.exp(s_pre - top)
        w_suf = jnp.exp(s_suf - top)
        total = jnp.sum(w_pre, axis=1, keepdims=True) + jnp.sum(w_suf, axis=1, keepdims=True)
        mixed = dot_nn(w_pre.astype(BF), v) + dot_nn(w_suf.astype(BF), vs)
        o_ref[slot, :, lanes] = jnp.where(live, mixed / total, 0.0).astype(BF)


def finish_kernel(
    pre_ref,
    suf_ref,
    want_ref,
    page_ref,
    q_ref,
    ks_ref,
    vs_ref,
    c_ref,
    p_ref,
    e_ref,
    bs_ref,
    dec_ref,
    gain_ref,
    mamba_ref,
    attn_ref,
    st_buf,
    kv_buf,
    o_buf,
    gated_buf,
    sum_buf,
    st_send,
    st_recv,
    kv_send,
    kv_recv,
    o_send,
    o_recv,
    sum_send,
    sum_recv,
):
    y = lax.axis_index("y")
    me = lax.axis_index("z") * 2 + lax.axis_index("core")

    barrier = pltpu.get_barrier_semaphore()

    def owner_id(k):
        other = lax.rem(me + k, 16)
        return other, {"z": other // 2, "core": lax.rem(other, 2)}

    def y_id(k):
        other = lax.rem(y + k, 4)
        return other, {"y": other}

    def greet(k, carry):
        pl.semaphore_signal(barrier, inc=1, device_id=owner_id(k)[1], device_id_type=MESH)
        return carry

    lax.fori_loop(1, 16, greet, 0)
    for k in range(1, 4):
        pl.semaphore_signal(barrier, inc=1, device_id=y_id(k)[1], device_id_type=MESH)
    pl.semaphore_wait(barrier, 18)

    def state_copy(k):
        other, device = owner_id(k)
        return pltpu.make_async_remote_copy(
            want_ref.at[other], st_buf.at[me], st_send.at[k], st_recv.at[k], device_id=device, device_id_type=MESH
        )

    def page_copy(k):
        other, device = y_id(k)
        return pltpu.make_async_remote_copy(
            page_ref.at[other], kv_buf.at[y], kv_send.at[k], kv_recv.at[k], device_id=device, device_id_type=MESH
        )

    def out_copy(k):
        other, device = y_id(k)
        return pltpu.make_async_remote_copy(
            o_buf.at[other], attn_ref.at[y], o_send.at[k], o_recv.at[k], device_id=device, device_id_type=MESH
        )

    def sum_copy(k):
        device = y_id(k)[1]
        return pltpu.make_async_remote_copy(
            sum_buf.at[y], sum_buf.at[y], sum_send.at[k], sum_recv.at[k], device_id=device, device_id_type=MESH
        )

    for k in (2, 1, 3):
        page_copy(k).start()

    def send_state(k, carry):
        state_copy(k).start()
        return carry

    lax.fori_loop(1, 16, send_state, 0)
    kv_buf[y] = page_ref[y]
    st_buf[me] = want_ref[me]
    for k in (1, 2, 3):
        page_copy(k).wait()

    request = me * REQ + y
    keys = MAXP * PAGE
    page = (lax.broadcasted_iota(jnp.int32, (1, keys), 1) // QUARTER) % MAXP
    bias = jnp.where(page * PAGE < pre_ref[request], 0.0, NEG)
    causal = lax.broadcasted_iota(jnp.int32, (SUF, SUF), 0) >= lax.broadcasted_iota(jnp.int32, (SUF, SUF), 1)
    live = lax.broadcasted_iota(jnp.int32, (SUF, HD), 0) < suf_ref[request]

    def attend_step(t, carry):
        kv = kv_buf[...].reshape(4 * MAXP, 2 * QUARTER, HD)
        k = kv[:, :QUARTER, :].reshape(keys, HD)
        v = kv[:, QUARTER:, :].reshape(keys, HD)
        slot = lax.rem(y + t, 4)
        attend_pair(q_ref, k, v, ks_ref[...], vs_ref[...], bias, causal, live, o_buf, slot)
        return carry

    lax.fori_loop(1, 5, attend_step, 0)
    for k in (1, 2, 3):
        out_copy(k).start()
    attn_ref[y] = o_buf[y]

    def wait_state(k, carry):
        state_copy(k).wait()
        return carry

    lax.fori_loop(1, 16, wait_state, 0)

    def mixer_step(j, carry):
        start = st_buf[:, j].reshape(CH, STATE)
        dec = dec_ref[j]
        begin = jnp.concatenate([dec, dec], axis=1) * start.astype(F32) + bs_ref[j]
        for blk, state in enumerate((start, begin.astype(BF))):
            rows = pl.ds(pl.multiple_of(j * SUF + blk * SPAN, SPAN), SPAN)
            carried = dot_nt(c_ref[rows, :], state)
            gated = p_ref[rows, :] + e_ref[rows, :] * carried
            gated_buf[rows, :] = gated
            total = jnp.sum(gated * gated, axis=1, keepdims=True)
            sum_buf[y, pl.ds(2 * j + blk, 1), :] = jnp.transpose(jnp.broadcast_to(total, (SPAN, SPAN)))[0:1, :]
        return carry

    lax.fori_loop(0, REQ, mixer_step, 0)
    for k in (2, 1, 3):
        sum_copy(k).start()
    for k in (1, 2, 3):
        sum_copy(k).wait()

    def norm_step(i, carry):
        rows = pl.ds(pl.multiple_of(i * SPAN, SPAN), SPAN)
        square = jnp.sum(sum_buf[:, pl.ds(i, 1), :], axis=0) / GROUP_CH
        factor = jnp.transpose(jnp.broadcast_to(lax.rsqrt(square + EPSILON), (SPAN, SPAN)))
        token = lax.broadcasted_iota(jnp.int32, (SPAN, SPAN), 0) + lax.rem(i, 2) * SPAN
        alive = token < suf_ref[me * REQ + i // 2]
        for part in range(CH // SPAN):
            lanes = pl.ds(part * SPAN, SPAN)
            value = gated_buf[rows, lanes] * factor * gain_ref[:, lanes]
            mamba_ref[rows, lanes] = jnp.where(alive, value, 0.0).astype(BF)
        return carry

    lax.fori_loop(0, 8, norm_step, 0)
    for k in (1, 2, 3):
        out_copy(k).wait()


def finish(prefix_len, suffix_len, wanted, mine, q, ks, vs, c, p, e, bs, dec, gain):
    vmem = pl.BlockSpec(memory_space=pltpu.VMEM)
    smem = pl.BlockSpec(memory_space=pltpu.SMEM)
    dma = pltpu.SemaphoreType.DMA
    return pl.pallas_call(
        finish_kernel,
        in_specs=[smem, smem] + [vmem] * 11,
        out_specs=[vmem, vmem],
        out_shape=[
            jax.ShapeDtypeStruct((REQ * SUF, CH), BF),
            jax.ShapeDtypeStruct((4, SUF, 2 * HD), BF),
        ],
        scratch_shapes=[
            pltpu.VMEM((16, REQ, CH // 16, STATE), BF),
            pltpu.VMEM((4, MAXP, 2 * QUARTER, HD), BF),
            pltpu.VMEM((4, SUF, 2 * HD), BF),
            pltpu.VMEM((REQ * SUF, CH), F32),
            pltpu.VMEM((4, 8, SPAN), F32),
            dma((16,)),
            dma((16,)),
            dma((4,)),
            dma((4,)),
            dma((4,)),
            dma((4,)),
            dma((4,)),
            dma((4,)),
        ],
        compiler_params=pltpu.CompilerParams(
            collective_id=0, has_side_effects=True, vmem_limit_bytes=40 << 20
        ),
        cost_estimate=pl.CostEstimate(flops=3_000_000_000, bytes_accessed=16 << 20, transcendentals=5 << 20),
        name="finish",
    )(prefix_len, suffix_len, wanted, mine, q, ks, vs, c, p, e, bs, dec, gain)


def cut_kernel(src_ref, dst_ref, sem):
    for k in range(16):
        pltpu.make_async_copy(src_ref.at[:, k], dst_ref.at[k], sem.at[k]).start()
    for k in range(16):
        pltpu.make_async_copy(src_ref.at[:, k], dst_ref.at[k], sem.at[k]).wait()


def cut_states(states):
    return pl.pallas_call(
        cut_kernel,
        in_specs=[pl.BlockSpec(memory_space=pltpu.VMEM)],
        out_specs=pl.BlockSpec(memory_space=pltpu.HBM),
        out_shape=jax.ShapeDtypeStruct((16, 4, CH // 16, STATE), BF),
        scratch_shapes=[pltpu.SemaphoreType.DMA((16,))],
        cost_estimate=pl.CostEstimate(flops=0, bytes_accessed=2 << 20, transcendentals=0),
        name="cut_states",
    )(states)


def pick_kernel(ho_ref, hs_ref, po_ref, ps_ref, base_ref, hop_ref, pool_ref, want_ref, mine_ref, sem):
    first = base_ref[0] * REQ * MAXP

    def begin(i, carry):
        pltpu.make_async_copy(hop_ref.at[ho_ref[i] * 4 + hs_ref[i]], want_ref.at[i], sem.at[0]).start()
        e = first + i
        pltpu.make_async_copy(pool_ref.at[po_ref[e] * 16 + ps_ref[e]], mine_ref.at[i], sem.at[1]).start()
        return carry

    lax.fori_loop(0, 64, begin, 0)
    pltpu.make_async_copy(hop_ref.at[pl.ds(0, 64)], want_ref, sem.at[0]).wait()
    pltpu.make_async_copy(pool_ref.at[pl.ds(0, 64)], mine_ref, sem.at[1]).wait()


def pick(hit_owner, hit_slot, page_owner, page_slot, base, hop, pool):
    smem = pl.BlockSpec(memory_space=pltpu.SMEM)
    hbm = pl.BlockSpec(memory_space=pltpu.HBM)
    vmem = pl.BlockSpec(memory_space=pltpu.VMEM)
    return pl.pallas_call(
        pick_kernel,
        in_specs=[smem] * 5 + [hbm, hbm],
        out_specs=[vmem, vmem],
        out_shape=[
            jax.ShapeDtypeStruct((64,) + hop.shape[1:], BF),
            jax.ShapeDtypeStruct((64,) + pool.shape[1:], BF),
        ],
        scratch_shapes=[pltpu.SemaphoreType.DMA((2,))],
        cost_estimate=pl.CostEstimate(flops=0, bytes_accessed=4 << 20, transcendentals=0),
        name="pick",
    )(hit_owner, hit_slot, page_owner, page_slot, base, hop, pool)


def body(
    mixer_input,
    step_raw,
    decay_rate,
    skip_gain,
    state_proj,
    queries,
    suffix_kv,
    state_pool,
    page_pool,
    norm_gain,
    hit_owner,
    hit_slot,
    page_owner,
    page_slot,
    prefix_len,
    suffix_len,
):
    owner_index = lax.axis_index("z") * 2 + lax.axis_index("core")
    x_index = lax.axis_index("x")
    y_index = lax.axis_index("y")
    tok = REQ * SUF

    piece = lax.dynamic_slice(
        page_pool, (0, y_index * QUARTER, 0, x_index, 0), (16, QUARTER, 2, 1, HD)
    ).reshape(16, QUARTER, 2, HD)
    piece = jnp.transpose(piece, (0, 2, 1, 3)).reshape(16, 2 * QUARTER, HD)
    pool = lax.all_gather(piece, OWN, axis=0, tiled=True)

    cut = cut_states(state_pool.reshape(4, 16, CH // 16, STATE))
    hop = lax.all_to_all(cut, OWN, split_axis=0, concat_axis=0, tiled=True)

    query = lax.all_to_all(queries.reshape(REQ, SUF, 2 * HD), "y", split_axis=0, concat_axis=0, tiled=True)

    x = mixer_input[:, 0]
    z = mixer_input[:, 1]
    maps = lax.dynamic_slice(state_proj, (0, 0, x_index, 0), (tok, 2, 1, STATE))
    b = maps[:, 0, 0]
    c = maps[:, 1, 0]
    skip = jnp.repeat(skip_gain, MHDIM)[None]
    p, e, bs, dec = mixer_local(x, z, step_raw.T, decay_rate[:, None], skip, b, c)

    own_kv = lax.dynamic_slice(suffix_kv, (y_index * SUF, 0, x_index, 0), (SUF, 2, 1, HD))

    wanted, mine = pick(
        hit_owner.reshape(-1),
        hit_slot,
        page_owner.reshape(-1),
        page_slot.reshape(-1),
        owner_index.astype(jnp.int32).reshape(1),
        hop.reshape(64, CH // 16, STATE),
        pool,
    )
    mamba_out, attn = finish(
        prefix_len,
        suffix_len,
        wanted.reshape(16, REQ, CH // 16, STATE),
        mine.reshape(REQ, MAXP, 2 * QUARTER, HD),
        query,
        own_kv[:, 0, 0],
        own_kv[:, 1, 0],
        c,
        p,
        e,
        bs,
        dec,
        norm_gain[None],
    )
    return (mamba_out, attn.reshape(tok, 2 * HD))


def solution(mesh):
    grid = Mesh(mesh.devices.reshape(8, 2, 4, 4), ("z", "core", "x", "y"))
    col = ("x", "y")
    return jax.shard_map(
        body,
        mesh=grid,
        in_specs=(
            P(OWN, None, col),
            P(OWN, col),
            P(col),
            P(col),
            P(OWN, None, None, None),
            P(OWN, col),
            P(OWN, None, None, None),
            P(OWN, col, None, None),
            P(OWN, None, None, None, None),
            P(col),
            P(),
            P(),
            P(),
            P(),
            P(),
            P(),
        ),
        out_specs=(P(OWN, col), P(OWN, col)),
        check_vma=False,
    )
```

```python
import functools
import math

import jax
import jax.numpy as jnp
from jax import lax
from jax.experimental import pallas as pl
from jax.experimental.pallas import tpu as pltpu
from jax.sharding import Mesh
from jax.sharding import PartitionSpec as P

HEADS = 8
MHDIM = 64
CH = HEADS * MHDIM
STATE = 256
GROUP_CH = 2048
HD = 128
PAGE = 128
SPAN = 128
SUF = 256
MAXP = 16
REQ = 4
QUARTER = PAGE // 4
EPSILON = 1e-05
NEG = -1e30
OWN = ("z", "core")
BF = jnp.bfloat16
F32 = jnp.float32
HI = lax.Precision.HIGHEST


def dot_nt(a, b):
    return lax.dot_general(a, b, (((1,), (1,)), ((), ())), preferred_element_type=F32)


def dot_nn(a, b):
    return lax.dot_general(a, b, (((1,), (0,)), ((), ())), preferred_element_type=F32)


def dot_tn(a, b):
    return lax.dot_general(a, b, (((0,), (0,)), ((), ())), preferred_element_type=F32)


def expand(cols):
    head = lax.broadcasted_iota(jnp.int32, (HEADS, CH), 0)
    chan = lax.broadcasted_iota(jnp.int32, (HEADS, CH), 1)
    pick = (chan // MHDIM == head).astype(F32)
    return lax.dot_general(
        cols, pick, (((1,), (0,)), ((), ())), preferred_element_type=F32, precision=HI
    )


MESH = pl.DeviceIdType.MESH


def attend_pair(q_ref, k, v, ks, vs, bias, causal, live, o_ref, slot):
    scale = 1.0 / math.sqrt(HD)
    for half in range(2):
        lanes = pl.ds(half * HD, HD)
        q = q_ref[slot, :, lanes]
        s_pre = dot_nt(q, k) * scale + bias
        s_suf = jnp.where(causal, dot_nt(q, ks) * scale, NEG)
        top = jnp.maximum(
            jnp.max(s_pre, axis=1, keepdims=True), jnp.max(s_suf, axis=1, keepdims=True)
        )
        w_pre = jnp.exp(s_pre - top)
        w_suf = jnp.exp(s_suf - top)
        total = jnp.sum(w_pre, axis=1, keepdims=True) + jnp.sum(w_suf, axis=1, keepdims=True)
        mixed = dot_nn(w_pre.astype(BF), v) + dot_nn(w_suf.astype(BF), vs)
        o_ref[slot, :, lanes] = jnp.where(live, mixed / total, 0.0).astype(BF)


def program_kernel(
    ho_ref,
    hs_ref,
    po_ref,
    ps_ref,
    pre_ref,
    suf_ref,
    decay_ref,
    skip_ref,
    mix_hbm,
    step_hbm,
    proj_hbm,
    query_hbm,
    suffix_hbm,
    state_hbm,
    page_hbm,
    gain_hbm,
    mamba_ref,
    attn_ref,
    mix_raw,
    step_buf,
    proj_raw,
    suf_raw,
    page_raw,
    gain_buf,
    q_buf,
    b_buf,
    c_buf,
    ks_buf,
    vs_buf,
    p_buf,
    e_buf,
    bs_buf,
    dec_buf,
    pool_buf,
    hop_buf,
    want_buf,
    mine_buf,
    st_buf,
    kv_buf,
    o_buf,
    sum_buf,
    load_sem,
    q_send,
    q_recv,
    hop_send,
    hop_recv,
    st_send,
    st_recv,
    right_send,
    right_recv,
    left_send,
    left_recv,
    sib_send,
    sib_recv,
    kv_send,
    kv_recv,
    o_send,
    o_recv,
    sum_send,
    sum_recv,
):
    x = lax.axis_index("x")
    y = lax.axis_index("y")
    z = lax.axis_index("z")
    core = lax.axis_index("core")
    me = z * 2 + core
    barrier = pltpu.get_barrier_semaphore()

    def owner_id(k):
        other = lax.rem(me + k, 16)
        return other, {"z": other // 2, "core": lax.rem(other, 2)}

    def y_id(k):
        other = lax.rem(y + k, 4)
        return other, {"y": other}

    def send(src, dst, send_sem, recv_sem, device):
        return pltpu.make_async_remote_copy(
            src, dst, send_sem, recv_sem, device_id=device, device_id_type=MESH
        )

    def q_copy(k):
        other, device = y_id(k)
        return send(query_hbm.at[other], q_buf.at[y], q_send.at[k], q_recv.at[k], device)

    def hop_copy(k):
        other, device = owner_id(k)
        return send(state_hbm.at[:, other], hop_buf.at[me], hop_send.at[k], hop_recv.at[k], device)

    def state_copy(k):
        other, device = owner_id(k)
        return send(want_buf.at[other], st_buf.at[me], st_send.at[k], st_recv.at[k], device)

    def right_copy(s):
        piece = lax.rem(z - s + 9, 8) * 2 + core
        ref = pool_buf.at[piece]
        return send(ref, ref, right_send.at[s], right_recv.at[s], {"z": lax.rem(z + 1, 8)})

    def left_copy(s):
        piece = lax.rem(z + s - 1, 8) * 2 + core
        ref = pool_buf.at[piece]
        return send(ref, ref, left_send.at[s], left_recv.at[s], {"z": lax.rem(z + 7, 8)})

    def right_last():
        piece = lax.rem(z + 5, 8) * 2 + core
        ref = pool_buf.at[piece, pl.ds(0, 8)]
        return send(ref, ref, right_send.at[4], right_recv.at[4], {"z": lax.rem(z + 1, 8)})

    def left_last():
        piece = lax.rem(z + 3, 8) * 2 + core
        ref = pool_buf.at[piece, pl.ds(8, 8)]
        return send(ref, ref, left_send.at[4], left_recv.at[4], {"z": lax.rem(z + 7, 8)})

    def sibling_copy(far, k):
        piece = lax.rem(z + far, 8) * 2 + core
        ref = pool_buf.at[piece]
        return send(ref, ref, sib_send.at[k], sib_recv.at[k], {"core": 1 - core})

    def page_copy(k):
        other, device = y_id(k)
        return send(mine_buf.at[other], kv_buf.at[y], kv_send.at[k], kv_recv.at[k], device)

    def out_copy(k):
        other, device = y_id(k)
        return send(o_buf.at[other], attn_ref.at[y], o_send.at[k], o_recv.at[k], device)

    def sum_copy(k):
        device = y_id(k)[1]
        return send(sum_buf.at[y], sum_buf.at[y], sum_send.at[k], sum_recv.at[k], device)

    load_pages = pltpu.make_async_copy(page_hbm.at[:, pl.ds(y * QUARTER, QUARTER)], page_raw, load_sem.at[0])
    load_proj = pltpu.make_async_copy(proj_hbm, proj_raw, load_sem.at[1])
    load_mix = pltpu.make_async_copy(mix_hbm, mix_raw, load_sem.at[2])
    load_step = pltpu.make_async_copy(step_hbm, step_buf, load_sem.at[3])
    load_suf = pltpu.make_async_copy(suffix_hbm.at[pl.ds(y * SUF, SUF)], suf_raw, load_sem.at[4])
    load_gain = pltpu.make_async_copy(gain_hbm, gain_buf, load_sem.at[5])
    load_q = pltpu.make_async_copy(query_hbm.at[y], q_buf.at[y], load_sem.at[6])
    load_hop = pltpu.make_async_copy(state_hbm.at[:, me], hop_buf.at[me], load_sem.at[7])
    load_pages.start()

    def greet(k, carry):
        pl.semaphore_signal(barrier, inc=1, device_id=owner_id(k)[1], device_id_type=MESH)
        return carry

    lax.fori_loop(1, 16, greet, 0)
    for k in range(1, 4):
        pl.semaphore_signal(barrier, inc=1, device_id=y_id(k)[1], device_id_type=MESH)
    for load in (load_proj, load_mix, load_step, load_suf, load_gain, load_q, load_hop):
        load.start()
    load_pages.wait()
    for head in range(4):

        @pl.when(x == head)
        def _(head=head):
            def extract(i, carry):
                pool_buf[me, i, 0:QUARTER, :] = page_raw[i, :, 0, head, :]
                pool_buf[me, i, QUARTER : 2 * QUARTER, :] = page_raw[i, :, 1, head, :]
                return carry

            lax.fori_loop(0, 16, extract, 0)

    pl.semaphore_wait(barrier, 18)
    right_copy(1).start()
    left_copy(1).start()
    sibling_copy(0, 0).start()

    def send_hop(k, carry):
        hop_copy(k).start()
        return carry

    lax.fori_loop(1, 16, send_hop, 0)
    for k in (2, 1, 3):
        q_copy(k).start()

    load_proj.wait()
    load_suf.wait()
    for head in range(4):

        @pl.when(x == head)
        def _(head=head):
            def extract(i, carry):
                rows = pl.ds(pl.multiple_of(i * 64, 64), 64)
                b_buf[rows, :] = proj_raw[rows, 0, head, :]
                c_buf[rows, :] = proj_raw[rows, 1, head, :]
                return carry

            lax.fori_loop(0, 16, extract, 0)
            ks_buf[...] = suf_raw[:, 0, head, :]
            vs_buf[...] = suf_raw[:, 1, head, :]

    load_mix.wait()
    load_step.wait()

    def mixer_local(j):
        lane = lax.broadcasted_iota(jnp.int32, (HEADS, SPAN), 1)
        head_row = lax.broadcasted_iota(jnp.int32, (HEADS, SPAN), 0)
        lower = lax.broadcasted_iota(jnp.int32, (SPAN, SPAN), 0) >= lax.broadcasted_iota(
            jnp.int32, (SPAN, SPAN), 1
        )
        low_half = lax.broadcasted_iota(jnp.int32, (SPAN, 2 * MHDIM), 1) < MHDIM
        decay = jnp.zeros((HEADS, SPAN), F32)
        for h in range(HEADS):
            decay = jnp.where(head_row == h, decay_ref[h], decay)
        for blk in range(SUF // SPAN):
            rows = pl.ds(pl.multiple_of(j * SUF + blk * SPAN, SPAN), SPAN)
            raw = step_buf[:, rows]
            rate = jnp.maximum(raw, 0.0) + jnp.log(1.0 + jnp.exp(-jnp.abs(raw)))
            cum = -rate * decay
            shift = 1
            while shift < SPAN:
                cum = cum + jnp.where(lane >= shift, pltpu.roll(cum, shift, 1), 0.0)
                shift *= 2
            cum_col = jnp.transpose(cum)
            xs = mix_raw[rows, 0, :]
            zs = mix_raw[rows, 1, :]
            b = b_buf[rows, :]
            inter = dot_nt(c_buf[rows, :], b)
            for pair in range(HEADS // 2):
                parts = []
                for h in (2 * pair, 2 * pair + 1):
                    gap = cum_col[:, h : h + 1] - cum[h : h + 1, :]
                    fade = jnp.exp(jnp.where(lower, gap, NEG))
                    parts.append((inter * fade * rate[h : h + 1, :]).astype(BF))
                lanes = slice(pair * 2 * MHDIM, (pair + 1) * 2 * MHDIM)
                xp = xs[:, lanes]
                inner = jnp.where(low_half, dot_nn(parts[0], xp), dot_nn(parts[1], xp))
                zp = zs[:, lanes].astype(F32)
                gate = zp / (1.0 + jnp.exp(-zp))
                skip = jnp.where(low_half, skip_ref[2 * pair], skip_ref[2 * pair + 1])
                p_buf[rows, lanes] = (inner + skip * xp.astype(F32)) * gate
                grow = jnp.where(
                    low_half,
                    jnp.broadcast_to(cum_col[:, 2 * pair : 2 * pair + 1], (SPAN, 2 * MHDIM)),
                    jnp.broadcast_to(cum_col[:, 2 * pair + 1 : 2 * pair + 2], (SPAN, 2 * MHDIM)),
                )
                e_buf[rows, lanes] = jnp.exp(grow) * gate
            if blk == 0:
                end = cum[:, SPAN - 1 : SPAN]
                tail = jnp.transpose(jnp.exp(end - cum) * rate)
                scaled = (expand(tail) * xs.astype(F32)).astype(BF)
                bs_buf[j] = dot_tn(scaled, b)
                keep = jnp.transpose(jnp.broadcast_to(jnp.exp(end), (HEADS, SPAN)))
                dec_buf[j] = jnp.transpose(expand(keep))

    def ring_step(s, carry):
        mixer_local(s - 1)
        right_copy(s).wait()
        left_copy(s).wait()

        @pl.when(s < 3)
        def _():
            right_copy(s + 1).start()
            left_copy(s + 1).start()

        @pl.when(s == 3)
        def _():
            right_last().start()
            left_last().start()

        sibling_copy(8 - s, 2 * s - 1).start()
        sibling_copy(s, 2 * s).start()
        return carry

    lax.fori_loop(1, 4, ring_step, 0)
    mixer_local(3)
    right_last().wait()
    left_last().wait()
    sibling_copy(4, 7).start()

    def wait_hop(k, carry):
        hop_copy(k).wait()
        return carry

    lax.fori_loop(1, 16, wait_hop, 0)
    load_hop.wait()

    def pick_state(i, carry):
        want_buf[i // REQ, lax.rem(i, REQ)] = hop_buf[ho_ref[i], hs_ref[i]]
        return carry

    lax.fori_loop(0, 64, pick_state, 0)

    def send_state(k, carry):
        state_copy(k).start()
        return carry

    lax.fori_loop(1, 16, send_state, 0)
    st_buf[me] = want_buf[me]

    def wait_sibling(k, carry):
        sibling_copy(0, k).wait()
        return carry

    lax.fori_loop(0, 8, wait_sibling, 0)

    def pick_page(i, carry):
        r = i // MAXP
        p = lax.rem(i, MAXP)
        mine_buf[r, p] = pool_buf[po_ref[p, me * REQ + r], ps_ref[p, me * REQ + r]]
        return carry

    lax.fori_loop(0, 64, pick_page, 0)
    for k in (2, 1, 3):
        page_copy(k).start()
    kv_buf[y] = mine_buf[y]
    for k in (1, 2, 3):
        q_copy(k).wait()
    load_q.wait()
    for k in (1, 2, 3):
        page_copy(k).wait()

    request = me * REQ + y
    keys = MAXP * PAGE
    page = (lax.broadcasted_iota(jnp.int32, (1, keys), 1) // QUARTER) % MAXP
    bias = jnp.where(page * PAGE < pre_ref[request], 0.0, NEG)
    causal = lax.broadcasted_iota(jnp.int32, (SUF, SUF), 0) >= lax.broadcasted_iota(jnp.int32, (SUF, SUF), 1)
    live = lax.broadcasted_iota(jnp.int32, (SUF, HD), 0) < suf_ref[request]

    def attend_step(t, carry):
        kv = kv_buf[...].reshape(4 * MAXP, 2 * QUARTER, HD)
        k = kv[:, :QUARTER, :].reshape(keys, HD)
        v = kv[:, QUARTER:, :].reshape(keys, HD)
        slot = lax.rem(y + t, 4)
        attend_pair(q_buf, k, v, ks_buf[...], vs_buf[...], bias, causal, live, o_buf, slot)

        @pl.when(t < 4)
        def _():
            out_copy(t).start()

        return carry

    lax.fori_loop(1, 5, attend_step, 0)
    attn_ref[y] = o_buf[y]

    def wait_state(k, carry):
        state_copy(k).wait()
        return carry

    lax.fori_loop(1, 16, wait_state, 0)

    def mixer_step(j, carry):
        start = st_buf[:, j].reshape(CH, STATE)
        dec = dec_buf[j]
        begin = jnp.concatenate([dec, dec], axis=1) * start.astype(F32) + bs_buf[j]
        for blk, state in enumerate((start, begin.astype(BF))):
            rows = pl.ds(pl.multiple_of(j * SUF + blk * SPAN, SPAN), SPAN)
            carried = dot_nt(c_buf[rows, :], state)
            gated = p_buf[rows, :] + e_buf[rows, :] * carried
            p_buf[rows, :] = gated
            total = jnp.sum(gated * gated, axis=1, keepdims=True)
            sum_buf[y, pl.ds(2 * j + blk, 1), :] = jnp.transpose(jnp.broadcast_to(total, (SPAN, SPAN)))[0:1, :]
        return carry

    lax.fori_loop(0, REQ, mixer_step, 0)
    for k in (2, 1, 3):
        sum_copy(k).start()
    load_gain.wait()
    for k in (1, 2, 3):
        sum_copy(k).wait()

    def norm_step(i, carry):
        rows = pl.ds(pl.multiple_of(i * SPAN, SPAN), SPAN)
        square = jnp.sum(sum_buf[:, pl.ds(i, 1), :], axis=0) / GROUP_CH
        factor = jnp.transpose(jnp.broadcast_to(lax.rsqrt(square + EPSILON), (SPAN, SPAN)))
        token = lax.broadcasted_iota(jnp.int32, (SPAN, SPAN), 0) + lax.rem(i, 2) * SPAN
        alive = token < suf_ref[me * REQ + i // 2]
        for part in range(CH // SPAN):
            lanes = pl.ds(part * SPAN, SPAN)
            value = p_buf[rows, lanes] * factor * gain_buf[:, lanes]
            mamba_ref[rows, lanes] = jnp.where(alive, value, 0.0).astype(BF)
        return carry

    lax.fori_loop(0, 8, norm_step, 0)
    for k in (1, 2, 3):
        out_copy(k).wait()


def run_program(scalars, arrays):
    vmem = pl.BlockSpec(memory_space=pltpu.VMEM)
    smem = pl.BlockSpec(memory_space=pltpu.SMEM)
    hbm = pl.BlockSpec(memory_space=pltpu.HBM)
    dma = pltpu.SemaphoreType.DMA
    tok = REQ * SUF
    return pl.pallas_call(
        program_kernel,
        in_specs=[smem] * len(scalars) + [hbm] * len(arrays),
        out_specs=[vmem, vmem],
        out_shape=[
            jax.ShapeDtypeStruct((tok, CH), BF),
            jax.ShapeDtypeStruct((4, SUF, 2 * HD), BF),
        ],
        scratch_shapes=[
            pltpu.VMEM((tok, 2, CH), BF),
            pltpu.VMEM((HEADS, tok), F32),
            pltpu.VMEM((tok, 2, 4, STATE), BF),
            pltpu.VMEM((SUF, 2, 4, HD), BF),
            pltpu.VMEM((16, QUARTER, 2, 4, HD), BF),
            pltpu.VMEM((1, CH), F32),
            pltpu.VMEM((4, SUF, 2 * HD), BF),
            pltpu.VMEM((tok, STATE), BF),
            pltpu.VMEM((tok, STATE), BF),
            pltpu.VMEM((SUF, HD), BF),
            pltpu.VMEM((SUF, HD), BF),
            pltpu.VMEM((tok, CH), F32),
            pltpu.VMEM((tok, CH), F32),
            pltpu.VMEM((REQ, CH, STATE), F32),
            pltpu.VMEM((REQ, CH, SPAN), F32),
            pltpu.VMEM((16, 16, 2 * QUARTER, HD), BF),
            pltpu.VMEM((16, 4, CH // 16, STATE), BF),
            pltpu.VMEM((16, REQ, CH // 16, STATE), BF),
            pltpu.VMEM((REQ, MAXP, 2 * QUARTER, HD), BF),
            pltpu.VMEM((16, REQ, CH // 16, STATE), BF),
            pltpu.VMEM((4, MAXP, 2 * QUARTER, HD), BF),
            pltpu.VMEM((4, SUF, 2 * HD), BF),
            pltpu.VMEM((4, 8, SPAN), F32),
            dma((8,)),
            dma((4,)),
            dma((4,)),
            dma((16,)),
            dma((16,)),
            dma((16,)),
            dma((16,)),
            dma((5,)),
            dma((5,)),
            dma((5,)),
            dma((5,)),
            dma((8,)),
            dma((8,)),
            dma((4,)),
            dma((4,)),
            dma((4,)),
            dma((4,)),
            dma((4,)),
            dma((4,)),
        ],
        compiler_params=pltpu.CompilerParams(
            collective_id=0, has_side_effects=True, vmem_limit_bytes=56 << 20
        ),
        cost_estimate=pl.CostEstimate(flops=5_000_000_000, bytes_accessed=16 << 20, transcendentals=8 << 20),
        name="prefill",
    )(*scalars, *arrays)


def body(
    mixer_input,
    step_raw,
    decay_rate,
    skip_gain,
    state_proj,
    queries,
    suffix_kv,
    state_pool,
    page_pool,
    norm_gain,
    hit_owner,
    hit_slot,
    page_owner,
    page_slot,
    prefix_len,
    suffix_len,
):
    scalars = (
        hit_owner.reshape(-1),
        hit_slot,
        page_owner[:, :, 0].T,
        page_slot.T,
        prefix_len,
        suffix_len,
        decay_rate,
        skip_gain,
    )
    arrays = (
        mixer_input,
        step_raw.T,
        state_proj,
        queries.reshape(REQ, SUF, 2 * HD),
        suffix_kv,
        state_pool.reshape(4, 16, CH // 16, STATE),
        page_pool,
        norm_gain[None],
    )
    mamba_out, attn = run_program(scalars, arrays)
    return (mamba_out, attn.reshape(REQ * SUF, 2 * HD))


def solution(mesh):
    grid = Mesh(mesh.devices.reshape(8, 2, 4, 4), ("z", "core", "x", "y"))
    col = ("x", "y")
    return jax.shard_map(
        body,
        mesh=grid,
        in_specs=(
            P(OWN, None, col),
            P(OWN, col),
            P(col),
            P(col),
            P(OWN, None, None, None),
            P(OWN, col),
            P(OWN, None, None, None),
            P(OWN, col, None, None),
            P(OWN, None, None, None, None),
            P(col),
            P(),
            P(),
            P(),
            P(),
            P(),
            P(),
        ),
        out_specs=(P(OWN, col), P(OWN, col)),
        check_vma=False,
    )
```

```python
import functools
import math

import jax
import jax.numpy as jnp
from jax import lax
from jax.experimental import pallas as pl
from jax.experimental.pallas import tpu as pltpu
from jax.sharding import Mesh
from jax.sharding import PartitionSpec as P

HEADS = 8
MHDIM = 64
CH = HEADS * MHDIM
STATE = 256
GROUP_CH = 2048
HD = 128
PAGE = 128
SPAN = 128
SUF = 256
MAXP = 16
REQ = 4
QUARTER = PAGE // 4
EPSILON = 1e-05
NEG = -1e30
OWN = ("z", "core")
BF = jnp.bfloat16
F32 = jnp.float32
HI = lax.Precision.HIGHEST


def dot_nt(a, b):
    return lax.dot_general(a, b, (((1,), (1,)), ((), ())), preferred_element_type=F32)


def dot_nn(a, b):
    return lax.dot_general(a, b, (((1,), (0,)), ((), ())), preferred_element_type=F32)


def dot_tn(a, b):
    return lax.dot_general(a, b, (((0,), (0,)), ((), ())), preferred_element_type=F32)


def expand(cols):
    head = lax.broadcasted_iota(jnp.int32, (HEADS, CH), 0)
    chan = lax.broadcasted_iota(jnp.int32, (HEADS, CH), 1)
    pick = (chan // MHDIM == head).astype(F32)
    return lax.dot_general(
        cols, pick, (((1,), (0,)), ((), ())), preferred_element_type=F32, precision=HI
    )


MESH = pl.DeviceIdType.MESH


def attend_pair(q_ref, k, v, ks, vs, bias, causal, live, o_ref, slot):
    scale = 1.0 / math.sqrt(HD)
    for half in range(2):
        lanes = pl.ds(half * HD, HD)
        q = q_ref[slot, :, lanes]
        s_pre = dot_nt(q, k) * scale + bias
        s_suf = jnp.where(causal, dot_nt(q, ks) * scale, NEG)
        top = jnp.maximum(
            jnp.max(s_pre, axis=1, keepdims=True), jnp.max(s_suf, axis=1, keepdims=True)
        )
        w_pre = jnp.exp(s_pre - top)
        w_suf = jnp.exp(s_suf - top)
        total = jnp.sum(w_pre, axis=1, keepdims=True) + jnp.sum(w_suf, axis=1, keepdims=True)
        mixed = dot_nn(w_pre.astype(BF), v) + dot_nn(w_suf.astype(BF), vs)
        o_ref[slot, :, lanes] = jnp.where(live, mixed / total, 0.0).astype(BF)


def program_kernel(
    ho_ref,
    hs_ref,
    po_ref,
    ps_ref,
    pre_ref,
    suf_ref,
    decay_ref,
    skip_ref,
    mix_hbm,
    step_hbm,
    proj_hbm,
    query_hbm,
    suffix_hbm,
    state_hbm,
    page_hbm,
    gain_hbm,
    mamba_ref,
    attn_ref,
    mix_raw,
    step_buf,
    proj_raw,
    suf_raw,
    page_raw,
    gain_buf,
    q_buf,
    b_buf,
    c_buf,
    ks_buf,
    vs_buf,
    p_buf,
    e_buf,
    bs_buf,
    dec_buf,
    pool_buf,
    hop_buf,
    want_buf,
    mine_buf,
    st_buf,
    kv_buf,
    o_buf,
    sum_buf,
    load_sem,
    q_send,
    q_recv,
    hop_send,
    hop_recv,
    st_send,
    st_recv,
    right_send,
    right_recv,
    left_send,
    left_recv,
    sib_send,
    sib_recv,
    kv_send,
    kv_recv,
    o_send,
    o_recv,
    sum_send,
    sum_recv,
):
    x = lax.axis_index("x")
    y = lax.axis_index("y")
    z = lax.axis_index("z")
    core = lax.axis_index("core")
    me = z * 2 + core
    barrier = pltpu.get_barrier_semaphore()

    def owner_id(k):
        other = lax.rem(me + k, 16)
        return other, {"z": other // 2, "core": lax.rem(other, 2)}

    def y_id(k):
        other = lax.rem(y + k, 4)
        return other, {"y": other}

    def send(src, dst, send_sem, recv_sem, device):
        return pltpu.make_async_remote_copy(
            src, dst, send_sem, recv_sem, device_id=device, device_id_type=MESH
        )

    def q_copy(k):
        other, device = y_id(k)
        return send(query_hbm.at[other], q_buf.at[y], q_send.at[k], q_recv.at[k], device)

    def hop_copy(k):
        other, device = owner_id(k)
        return send(state_hbm.at[:, other], hop_buf.at[me], hop_send.at[k], hop_recv.at[k], device)

    def state_copy(k):
        other, device = owner_id(k)
        return send(want_buf.at[other], st_buf.at[me], st_send.at[k], st_recv.at[k], device)

    def right_copy(s):
        piece = lax.rem(z - s + 9, 8) * 2 + core
        ref = pool_buf.at[piece]
        return send(ref, ref, right_send.at[s], right_recv.at[s], {"z": lax.rem(z + 1, 8)})

    def left_copy(s):
        piece = lax.rem(z + s - 1, 8) * 2 + core
        ref = pool_buf.at[piece]
        return send(ref, ref, left_send.at[s], left_recv.at[s], {"z": lax.rem(z + 7, 8)})

    def right_last():
        piece = lax.rem(z + 5, 8) * 2 + core
        ref = pool_buf.at[piece, pl.ds(0, 8)]
        return send(ref, ref, right_send.at[4], right_recv.at[4], {"z": lax.rem(z + 1, 8)})

    def left_last():
        piece = lax.rem(z + 3, 8) * 2 + core
        ref = pool_buf.at[piece, pl.ds(8, 8)]
        return send(ref, ref, left_send.at[4], left_recv.at[4], {"z": lax.rem(z + 7, 8)})

    def sibling_copy(far, k):
        piece = lax.rem(z + far, 8) * 2 + core
        ref = pool_buf.at[piece]
        return send(ref, ref, sib_send.at[k], sib_recv.at[k], {"core": 1 - core})

    def page_copy(k):
        other, device = y_id(k)
        return send(mine_buf.at[other], kv_buf.at[y], kv_send.at[k], kv_recv.at[k], device)

    def out_copy(k):
        other, device = y_id(k)
        return send(o_buf.at[other], attn_ref.at[y], o_send.at[k], o_recv.at[k], device)

    def sum_copy(k):
        device = y_id(k)[1]
        return send(sum_buf.at[y], sum_buf.at[y], sum_send.at[k], sum_recv.at[k], device)

    load_pages = pltpu.make_async_copy(page_hbm.at[:, pl.ds(y * QUARTER, QUARTER)], page_raw, load_sem.at[0])
    load_proj = pltpu.make_async_copy(proj_hbm, proj_raw, load_sem.at[1])
    load_mix = pltpu.make_async_copy(mix_hbm, mix_raw, load_sem.at[2])
    load_step = pltpu.make_async_copy(step_hbm, step_buf, load_sem.at[3])
    load_suf = pltpu.make_async_copy(suffix_hbm.at[pl.ds(y * SUF, SUF)], suf_raw, load_sem.at[4])
    load_gain = pltpu.make_async_copy(gain_hbm, gain_buf, load_sem.at[5])
    load_q = pltpu.make_async_copy(query_hbm.at[y], q_buf.at[y], load_sem.at[6])
    load_hop = pltpu.make_async_copy(state_hbm.at[:, me], hop_buf.at[me], load_sem.at[7])
    load_pages.start()

    def greet(k, carry):
        pl.semaphore_signal(barrier, inc=1, device_id=owner_id(k)[1], device_id_type=MESH)
        return carry

    lax.fori_loop(1, 16, greet, 0)
    for k in range(1, 4):
        pl.semaphore_signal(barrier, inc=1, device_id=y_id(k)[1], device_id_type=MESH)
    for load in (load_proj, load_mix, load_step, load_suf, load_gain, load_q, load_hop):
        load.start()
    load_pages.wait()
    for head in range(4):

        @pl.when(x == head)
        def _(head=head):
            def extract(i, carry):
                pool_buf[me, i, 0:QUARTER, :] = page_raw[i, :, 0, head, :]
                pool_buf[me, i, QUARTER : 2 * QUARTER, :] = page_raw[i, :, 1, head, :]
                return carry

            lax.fori_loop(0, 16, extract, 0)

    pl.semaphore_wait(barrier, 18)
    right_copy(1).start()
    left_copy(1).start()
    sibling_copy(0, 0).start()

    def send_hops(group):
        def send_hop(i, carry):
            hop_copy(lax.rem(group + 1, 3) * 5 + 1 + i).start()
            return carry

        lax.fori_loop(0, 5, send_hop, 0)

    send_hops(0)
    for k in (2, 1, 3):
        q_copy(k).start()

    load_proj.wait()
    load_suf.wait()
    for head in range(4):

        @pl.when(x == head)
        def _(head=head):
            def extract(i, carry):
                rows = pl.ds(pl.multiple_of(i * 64, 64), 64)
                b_buf[rows, :] = proj_raw[rows, 0, head, :]
                c_buf[rows, :] = proj_raw[rows, 1, head, :]
                return carry

            lax.fori_loop(0, 16, extract, 0)
            ks_buf[...] = suf_raw[:, 0, head, :]
            vs_buf[...] = suf_raw[:, 1, head, :]

    load_mix.wait()
    load_step.wait()

    def mixer_local(j):
        lane = lax.broadcasted_iota(jnp.int32, (HEADS, SPAN), 1)
        head_row = lax.broadcasted_iota(jnp.int32, (HEADS, SPAN), 0)
        lower = lax.broadcasted_iota(jnp.int32, (SPAN, SPAN), 0) >= lax.broadcasted_iota(
            jnp.int32, (SPAN, SPAN), 1
        )
        low_half = lax.broadcasted_iota(jnp.int32, (SPAN, 2 * MHDIM), 1) < MHDIM
        decay = jnp.zeros((HEADS, SPAN), F32)
        for h in range(HEADS):
            decay = jnp.where(head_row == h, decay_ref[h], decay)
        for blk in range(SUF // SPAN):
            rows = pl.ds(pl.multiple_of(j * SUF + blk * SPAN, SPAN), SPAN)
            raw = step_buf[:, rows]
            rate = jnp.maximum(raw, 0.0) + jnp.log(1.0 + jnp.exp(-jnp.abs(raw)))
            cum = -rate * decay
            shift = 1
            while shift < SPAN:
                cum = cum + jnp.where(lane >= shift, pltpu.roll(cum, shift, 1), 0.0)
                shift *= 2
            cum_col = jnp.transpose(cum)
            xs = mix_raw[rows, 0, :]
            zs = mix_raw[rows, 1, :]
            b = b_buf[rows, :]
            inter = dot_nt(c_buf[rows, :], b)
            for pair in range(HEADS // 2):
                parts = []
                for h in (2 * pair, 2 * pair + 1):
                    gap = cum_col[:, h : h + 1] - cum[h : h + 1, :]
                    fade = jnp.exp(jnp.where(lower, gap, NEG))
                    parts.append((inter * fade * rate[h : h + 1, :]).astype(BF))
                lanes = slice(pair * 2 * MHDIM, (pair + 1) * 2 * MHDIM)
                xp = xs[:, lanes]
                inner = jnp.where(low_half, dot_nn(parts[0], xp), dot_nn(parts[1], xp))
                zp = zs[:, lanes].astype(F32)
                gate = zp / (1.0 + jnp.exp(-zp))
                skip = jnp.where(low_half, skip_ref[2 * pair], skip_ref[2 * pair + 1])
                p_buf[rows, lanes] = (inner + skip * xp.astype(F32)) * gate
                grow = jnp.where(
                    low_half,
                    jnp.broadcast_to(cum_col[:, 2 * pair : 2 * pair + 1], (SPAN, 2 * MHDIM)),
                    jnp.broadcast_to(cum_col[:, 2 * pair + 1 : 2 * pair + 2], (SPAN, 2 * MHDIM)),
                )
                e_buf[rows, lanes] = jnp.exp(grow) * gate
            if blk == 0:
                end = cum[:, SPAN - 1 : SPAN]
                tail = jnp.transpose(jnp.exp(end - cum) * rate)
                scaled = (expand(tail) * xs.astype(F32)).astype(BF)
                bs_buf[j] = dot_tn(scaled, b)
                keep = jnp.transpose(jnp.broadcast_to(jnp.exp(end), (HEADS, SPAN)))
                dec_buf[j] = jnp.transpose(expand(keep))

    def ring_step(s, carry):
        mixer_local(s - 1)
        right_copy(s).wait()
        left_copy(s).wait()

        @pl.when(s < 3)
        def _():
            right_copy(s + 1).start()
            left_copy(s + 1).start()
            send_hops(s)

        @pl.when(s == 3)
        def _():
            right_last().start()
            left_last().start()

        sibling_copy(8 - s, 2 * s - 1).start()
        sibling_copy(s, 2 * s).start()
        return carry

    lax.fori_loop(1, 4, ring_step, 0)
    mixer_local(3)
    right_last().wait()
    left_last().wait()
    sibling_copy(4, 7).start()

    def wait_sibling(k, carry):
        sibling_copy(0, k).wait()
        return carry

    lax.fori_loop(0, 8, wait_sibling, 0)

    def pick_page(i, carry):
        r = i // MAXP
        p = lax.rem(i, MAXP)
        mine_buf[r, p] = pool_buf[po_ref[p, me * REQ + r], ps_ref[p, me * REQ + r]]
        return carry

    lax.fori_loop(0, 64, pick_page, 0)
    for k in (2, 1, 3):
        page_copy(k).start()
    def wait_hop(k, carry):
        hop_copy(k).wait()
        return carry

    lax.fori_loop(1, 16, wait_hop, 0)
    load_hop.wait()

    def pick_state(i, carry):
        want_buf[i // REQ, lax.rem(i, REQ)] = hop_buf[ho_ref[i], hs_ref[i]]
        return carry

    lax.fori_loop(0, 64, pick_state, 0)

    def send_state(k, carry):
        state_copy(k).start()
        return carry

    lax.fori_loop(1, 16, send_state, 0)
    st_buf[me] = want_buf[me]

    kv_buf[y] = mine_buf[y]
    for k in (1, 2, 3):
        q_copy(k).wait()
    load_q.wait()
    for k in (1, 2, 3):
        page_copy(k).wait()

    request = me * REQ + y
    keys = MAXP * PAGE
    page = (lax.broadcasted_iota(jnp.int32, (1, keys), 1) // QUARTER) % MAXP
    bias = jnp.where(page * PAGE < pre_ref[request], 0.0, NEG)
    causal = lax.broadcasted_iota(jnp.int32, (SUF, SUF), 0) >= lax.broadcasted_iota(jnp.int32, (SUF, SUF), 1)
    live = lax.broadcasted_iota(jnp.int32, (SUF, HD), 0) < suf_ref[request]

    def attend_step(t, carry):
        kv = kv_buf[...].reshape(4 * MAXP, 2 * QUARTER, HD)
        k = kv[:, :QUARTER, :].reshape(keys, HD)
        v = kv[:, QUARTER:, :].reshape(keys, HD)
        slot = lax.rem(y + t, 4)
        attend_pair(q_buf, k, v, ks_buf[...], vs_buf[...], bias, causal, live, o_buf, slot)

        @pl.when(t < 4)
        def _():
            out_copy(t).start()

        return carry

    lax.fori_loop(1, 5, attend_step, 0)
    attn_ref[y] = o_buf[y]

    def wait_state(k, carry):
        state_copy(k).wait()
        return carry

    lax.fori_loop(1, 16, wait_state, 0)

    def mixer_step(j, carry):
        start = st_buf[:, j].reshape(CH, STATE)
        dec = dec_buf[j]
        begin = jnp.concatenate([dec, dec], axis=1) * start.astype(F32) + bs_buf[j]
        for blk, state in enumerate((start, begin.astype(BF))):
            rows = pl.ds(pl.multiple_of(j * SUF + blk * SPAN, SPAN), SPAN)
            carried = dot_nt(c_buf[rows, :], state)
            gated = p_buf[rows, :] + e_buf[rows, :] * carried
            p_buf[rows, :] = gated
            total = jnp.sum(gated * gated, axis=1, keepdims=True)
            sum_buf[y, pl.ds(2 * j + blk, 1), :] = jnp.transpose(jnp.broadcast_to(total, (SPAN, SPAN)))[0:1, :]
        return carry

    lax.fori_loop(0, REQ, mixer_step, 0)
    for k in (2, 1, 3):
        sum_copy(k).start()
    load_gain.wait()
    for k in (1, 2, 3):
        sum_copy(k).wait()

    def norm_step(i, carry):
        rows = pl.ds(pl.multiple_of(i * SPAN, SPAN), SPAN)
        square = jnp.sum(sum_buf[:, pl.ds(i, 1), :], axis=0) / GROUP_CH
        factor = jnp.transpose(jnp.broadcast_to(lax.rsqrt(square + EPSILON), (SPAN, SPAN)))
        token = lax.broadcasted_iota(jnp.int32, (SPAN, SPAN), 0) + lax.rem(i, 2) * SPAN
        alive = token < suf_ref[me * REQ + i // 2]
        for part in range(CH // SPAN):
            lanes = pl.ds(part * SPAN, SPAN)
            value = p_buf[rows, lanes] * factor * gain_buf[:, lanes]
            mamba_ref[rows, lanes] = jnp.where(alive, value, 0.0).astype(BF)
        return carry

    lax.fori_loop(0, 8, norm_step, 0)
    for k in (1, 2, 3):
        out_copy(k).wait()


def run_program(scalars, arrays):
    vmem = pl.BlockSpec(memory_space=pltpu.VMEM)
    smem = pl.BlockSpec(memory_space=pltpu.SMEM)
    hbm = pl.BlockSpec(memory_space=pltpu.HBM)
    dma = pltpu.SemaphoreType.DMA
    tok = REQ * SUF
    return pl.pallas_call(
        program_kernel,
        in_specs=[smem] * len(scalars) + [hbm] * len(arrays),
        out_specs=[vmem, vmem],
        out_shape=[
            jax.ShapeDtypeStruct((tok, CH), BF),
            jax.ShapeDtypeStruct((4, SUF, 2 * HD), BF),
        ],
        scratch_shapes=[
            pltpu.VMEM((tok, 2, CH), BF),
            pltpu.VMEM((HEADS, tok), F32),
            pltpu.VMEM((tok, 2, 4, STATE), BF),
            pltpu.VMEM((SUF, 2, 4, HD), BF),
            pltpu.VMEM((16, QUARTER, 2, 4, HD), BF),
            pltpu.VMEM((1, CH), F32),
            pltpu.VMEM((4, SUF, 2 * HD), BF),
            pltpu.VMEM((tok, STATE), BF),
            pltpu.VMEM((tok, STATE), BF),
            pltpu.VMEM((SUF, HD), BF),
            pltpu.VMEM((SUF, HD), BF),
            pltpu.VMEM((tok, CH), F32),
            pltpu.VMEM((tok, CH), F32),
            pltpu.VMEM((REQ, CH, STATE), F32),
            pltpu.VMEM((REQ, CH, SPAN), F32),
            pltpu.VMEM((16, 16, 2 * QUARTER, HD), BF),
            pltpu.VMEM((16, 4, CH // 16, STATE), BF),
            pltpu.VMEM((16, REQ, CH // 16, STATE), BF),
            pltpu.VMEM((REQ, MAXP, 2 * QUARTER, HD), BF),
            pltpu.VMEM((16, REQ, CH // 16, STATE), BF),
            pltpu.VMEM((4, MAXP, 2 * QUARTER, HD), BF),
            pltpu.VMEM((4, SUF, 2 * HD), BF),
            pltpu.VMEM((4, 8, SPAN), F32),
            dma((8,)),
            dma((4,)),
            dma((4,)),
            dma((16,)),
            dma((16,)),
            dma((16,)),
            dma((16,)),
            dma((5,)),
            dma((5,)),
            dma((5,)),
            dma((5,)),
            dma((8,)),
            dma((8,)),
            dma((4,)),
            dma((4,)),
            dma((4,)),
            dma((4,)),
            dma((4,)),
            dma((4,)),
        ],
        compiler_params=pltpu.CompilerParams(
            collective_id=0, has_side_effects=True, vmem_limit_bytes=56 << 20
        ),
        cost_estimate=pl.CostEstimate(flops=5_000_000_000, bytes_accessed=16 << 20, transcendentals=8 << 20),
        name="prefill",
    )(*scalars, *arrays)


def body(
    mixer_input,
    step_raw,
    decay_rate,
    skip_gain,
    state_proj,
    queries,
    suffix_kv,
    state_pool,
    page_pool,
    norm_gain,
    hit_owner,
    hit_slot,
    page_owner,
    page_slot,
    prefix_len,
    suffix_len,
):
    scalars = (
        hit_owner.reshape(-1),
        hit_slot,
        page_owner[:, :, 0].T,
        page_slot.T,
        prefix_len,
        suffix_len,
        decay_rate,
        skip_gain,
    )
    arrays = (
        mixer_input,
        step_raw.T,
        state_proj,
        queries.reshape(REQ, SUF, 2 * HD),
        suffix_kv,
        state_pool.reshape(4, 16, CH // 16, STATE),
        page_pool,
        norm_gain[None],
    )
    mamba_out, attn = run_program(scalars, arrays)
    return (mamba_out, attn.reshape(REQ * SUF, 2 * HD))


def solution(mesh):
    grid = Mesh(mesh.devices.reshape(8, 2, 4, 4), ("z", "core", "x", "y"))
    col = ("x", "y")
    return jax.shard_map(
        body,
        mesh=grid,
        in_specs=(
            P(OWN, None, col),
            P(OWN, col),
            P(col),
            P(col),
            P(OWN, None, None, None),
            P(OWN, col),
            P(OWN, None, None, None),
            P(OWN, col, None, None),
            P(OWN, None, None, None, None),
            P(col),
            P(),
            P(),
            P(),
            P(),
            P(),
            P(),
        ),
        out_specs=(P(OWN, col), P(OWN, col)),
        check_vma=False,
    )
```
